32 devices in a mesh: gx: 8 (over y, x, core), gy: 4 (over z).
Axes of the slice: x: 2, y: 2, z: 4, core: 2. Of those that a mesh axis runs over, the one named last changes fastest.
Arguments:
- modes: float32 [3, 64, 8192], P(None, None, ('gx', 'gy')), may hold values from -6 to 6
- weights: float32 [8192], P(('gx', 'gy')), may hold values from 0.25 to 4
Outputs:
- tensor: float32 [64, 64, 64], P('gx', 'gy')
The draws below stay inside these ranges and needn't reach their ends.
All inputs are finite; a program needn't handle non-finite values.
Results may differ from the reference program's by a relative error of at most 0.00018.
Values sent between devices are 32-bit elements; how exact they have to be, the bound alone decides.
A program may use at most 64 MiB of HBM per device.

```python
import math
import jax
import jax.numpy as jnp
from jax import lax

M = 64
NZ = 128
NX = 8
NY = 8
NCELLS = 8192


def steps_of(stream_key, shape, split, smallest, high):
    loudness, own = 1.0, jax.random.fold_in(stream_key, 6)
    for dim, shards_of in split:
        steps = jnp.exp(jax.random.uniform(jax.random.fold_in(own, dim), (shards_of,), jnp.float32, smallest / len(split), high / len(split)))
        loudness = loudness * jnp.repeat(steps, shape[dim] // shards_of).reshape([-1 if axis == dim else 1 for axis in range(len(shape))])
    return loudness


def bell_draw(key, shape, width, reach, split=(), kind=jnp.bfloat16):
    level = steps_of(key, shape, split, -0.22, 0.18) if split else 1.0
    values = jax.random.normal(key, shape, jnp.float32) * width * level
    return jnp.minimum(jnp.maximum(values, -reach), reach).astype(kind)


def setup_inputs(seed: int = 0) -> dict:
    key_list = jax.random.split(jax.random.key(seed), 3)
    return {
        "modes": bell_draw(key_list[0], (3, M, NCELLS), 1.0, 6.0, ((2, 32),), jnp.float32),
        "weights": jnp.clip(jnp.exp(math.log(4.0) - 2.7725887 * jax.random.uniform(key_list[1], (NCELLS,), jnp.float32) ** steps_of(key_list[1], (NCELLS,), ((0, 32),), -0.2, 0.2)), 0.25, 4.0),
    }


def differences(field, upper, lower):
    grad_x = (upper - lower) * 0.5
    grad_y = (jnp.roll(field, -1, axis=2) - jnp.roll(field, 1, axis=2)) * 0.5
    grad_z = (jnp.roll(field, -1, axis=3) - jnp.roll(field, 1, axis=3)) * 0.5
    return [grad_x, grad_y, grad_z]

def contribution(field, grads, weighted):
    weighted_field = field * weighted
    result = jnp.zeros((field.shape[1], field.shape[1], field.shape[1]), jnp.float32)
    for comp_a in range(3):
        inner = field[0][:, None, :] * grads[0][comp_a][None, :, :]
        inner = inner + field[1][:, None, :] * grads[1][comp_a][None, :, :]
        inner = inner + field[2][:, None, :] * grads[2][comp_a][None, :, :]
        result = result + jnp.einsum('ic,jkc->ijk', weighted_field[comp_a], inner, precision=lax.Precision.HIGHEST)
    return result

def reference(modes, weights):
    mode_count = modes.shape[1]
    grid = modes.reshape(3, mode_count, NZ, NY, NX).transpose(0, 1, 4, 3, 2)
    weight_grid = weights.reshape(NZ, NY, NX).transpose(2, 1, 0)
    factor = 1.0 / math.sqrt(NX * NY * NZ)
    padded = jnp.concatenate([grid[:, :, -1:], grid, grid[:, :, :1]], axis=2)

    def plane(total, position):
        slab = lax.dynamic_slice_in_dim(padded, position, 3, axis=2)
        field = slab[:, :, 1]
        grads = differences(field, slab[:, :, 2], slab[:, :, 0])
        weight_row = lax.dynamic_index_in_dim(weight_grid, position, 0, keepdims=False) * factor
        flat = field.reshape(3, mode_count, -1)
        flat_grads = [g.reshape(3, mode_count, -1) for g in grads]
        return (total + contribution(flat, flat_grads, weight_row.reshape(-1)), None)
    total, _ = lax.scan(plane, jnp.zeros((mode_count, mode_count, mode_count), jnp.float32), jnp.arange(NX, dtype=jnp.int32))
    return total
```

```python
import functools
import math

import jax
import jax.numpy as jnp
from jax import lax
from jax.experimental import pallas as pl
from jax.experimental.pallas import tpu as pltpu
from jax.sharding import PartitionSpec as P

CX = 1
CY = 2
LANES = 128
ROWS = 16
UNIT = 4
MESH = pl.DeviceIdType.MESH


def partner_of(gx):
    return gx + 1 - 2 * (gx % 2)


def split(value):
    high = value.astype(jnp.bfloat16)
    low = (value - high.astype(jnp.float32)).astype(jnp.bfloat16)
    return high, low


def sizes(nx, ny, modes, cells):
    width, height = CX * nx, CY * ny
    plane = width * height
    own_i = modes // nx
    unit = UNIT if own_i % UNIT == 0 else own_i
    stages = 3 if cells > plane else 2
    return width, height, plane, max(1, LANES // plane), unit, own_i // unit, stages


def kernel(
    nx, ny, modes, factor,
    x_ref, w_ref, out_ref,
    other_x, other_w, edges, halos, weighted, diffs, field, sums, landed, line, line_in,
    near_send, near_recv, far_send, far_recv, line_send, line_recv,
):
    rows, cells = x_ref.shape
    width, height, plane, pack, unit, halves, stages = sizes(nx, ny, modes, cells)
    chips = nx // 2
    devices = nx * ny
    own_j = modes // ny
    early = stages * cells
    part = rows // pack
    gx, gy = lax.axis_index("gx"), lax.axis_index("gy")
    core, place = gx % 2, gx // 2
    mate = (partner_of(gx), gy)
    minor = 2 - chips % 2
    major = chips // minor

    def shifted(s):
        return (place // minor + s // minor) % major * minor + (place % minor + s % minor) % minor

    def beside(step, x, y):
        other = (x * ny + y + step + devices) % devices
        return other // ny, other % ny

    after = beside(1, gx, gy)
    after_mate = (partner_of(after[0]), after[1])
    before = beside(-1, gx, gy)
    before_mate = beside(-1, *mate)

    barrier = pltpu.get_barrier_semaphore()
    greeted = [mate, before, before_mate]
    greeted += [(shifted(s) * 2 + core, gy) for s in range(1, chips)]
    greeted += [(gx, (gy + t) % ny) for t in range(1, ny)]
    for device in greeted:
        pl.semaphore_signal(barrier, inc=1, device_id=device, device_id_type=MESH)

    def turned(value, step):
        span = value.shape[1]
        shift = (-step) % span
        return pltpu.roll(value, shift, 1) if shift else value

    start = cells - plane
    if pack == 1:
        edges[:rows] = x_ref[:, start:]
        edges[rows:] = jnp.broadcast_to(w_ref[:, start:], (8, plane))
    else:
        base = start // LANES * LANES
        lane = lax.broadcasted_iota(jnp.int32, (part, LANES), 1)
        packed = jnp.zeros((part, LANES), jnp.float32)
        for p in range(pack):
            piece = turned(x_ref[p * part : (p + 1) * part, base : base + LANES], start - base - p * plane)
            packed = jnp.where(lane // plane == p, piece, packed)
        edges[:part] = packed
        edges[part:] = jnp.broadcast_to(turned(w_ref[:, base : base + LANES], start - base), (8, LANES))

    def near(index, src, dst, device):
        return pltpu.make_async_remote_copy(
            src_ref=src, dst_ref=dst, send_sem=near_send.at[index], recv_sem=near_recv.at[index],
            device_id=device, device_id_type=MESH,
        )

    copies = [
        near(0, w_ref, other_w, mate),
        near(1, x_ref, other_x, mate),
        near(2, edges, halos.at[0], after),
        near(3, edges, halos.at[1], after_mate),
    ]
    pl.semaphore_wait(barrier, len(greeted))
    for index in (1, 0, 2, 3):
        copies[index].start()

    span = max(plane, LANES)
    lane = lax.broadcasted_iota(jnp.int32, (modes, span), 1)
    at_x, at_y = lane % width, lane // width % height
    whole = lax.broadcasted_iota(jnp.int32, (modes, cells), 1)

    def keep(a, value, weight, scale_at, field_at):
        size = value.shape[1]
        scaled = value * weight
        for n in range(nx * halves):
            weighted[n, a, :, scale_at : scale_at + size] = scaled[n * unit : (n + 1) * unit]
        for at in field_at:
            high, low = split(value)
            field[:modes, at : at + size] = high
            field[modes:, at : at + size] = low

    def prepare(which, ref, weight_ref):
        for a in range(3):
            for c in range(0, cells, span):
                value = ref[a * modes : (a + 1) * modes, c : c + span]
                at = which * early + c
                weight = weight_ref[:, c : c + span] * factor
                keep(a, value, weight, which * cells + c, [at + a * cells] if a < stages else [])
                up = jnp.where(at_x == width - 1, turned(value, 1 - width), turned(value, 1))
                down = jnp.where(at_x == 0, turned(value, width - 1), turned(value, -1))
                diffs[a, :, at : at + span] = (up - down) * 0.5
                turn = (height - 1) * width
                up = jnp.where(at_y == height - 1, turned(value, -turn), turned(value, width))
                down = jnp.where(at_y == 0, turned(value, turn), turned(value, -width))
                diffs[a, :, at + cells : at + cells + span] = (up - down) * 0.5
            if stages == 3:
                value = ref[a * modes : (a + 1) * modes, :]
                up = jnp.where(whole < cells - plane, turned(value, plane), 0.0)
                down = jnp.where(whole >= plane, turned(value, -plane), 0.0)
                at = which * early + 2 * cells
                diffs[a, :, at : at + cells] = (up - down) * 0.5

    def prepare_late(which, ref, weight_ref):
        at, scale_at = 2 * early + which * 2 * plane, 2 * cells + which * 2 * plane
        if pack == 1:
            for a in range(3):
                mine = slice(a * modes, (a + 1) * modes)
                own, halo = ref[mine, :plane], halos[which, mine, :]
                for value, other, weight, step in (
                    (own, halo * -0.5, weight_ref[:, :plane], 0),
                    (halo, own * 0.5, halos[which, rows : rows + 1, :], plane),
                ):
                    keep(a, value, weight * factor, scale_at + step, [at + step] if a == 2 else [])
                    diffs[a, :, at + step : at + step + plane] = other
            return
        narrow = lax.broadcasted_iota(jnp.int32, (8, LANES), 1)
        low_part = narrow < plane
        weight = jnp.where(low_part[:1], weight_ref[:, :LANES], turned(halos[which, part : part + 1, :], -plane))
        for a in range(3):
            values = []
            for r in range(0, modes, 8):
                q = a * modes + r
                own = ref[q : q + 8, :LANES]
                halo = halos[which, q % part : q % part + 8, :]
                halo = turned(halo, (q // part - 1) * plane)
                values.append(jnp.where(low_part, own, halo))
                diffs[a, r : r + 8, at : at + LANES] = turned(jnp.where(low_part, own, -halo), plane) * 0.5
            keep(a, jnp.concatenate(values, axis=0), weight * factor, scale_at, [at] if a == 2 else [])

    dims = (((1,), (1,)), ((), ()))
    first = [
        [(which * early + b * cells + c, which * cells + c) for b in range(stages) for c in range(0, cells, LANES)]
        for which in range(2)
    ]
    late = [(2 * early + c, 2 * cells + c) for c in range(0, 4 * plane, LANES)]

    def block(s, half, tiles, fresh):
        group = (shifted(s) * 2 + core) * halves + half
        highs, lows = [], []
        for i in range(unit):
            for k in range(0, modes, ROWS):
                pieces = []
                for at, scale_at in tiles:
                    scales = [
                        weighted[group, a, i : i + 1, scale_at : scale_at + LANES] for a in range(3)
                    ]
                    value = scales[0] * diffs[0, k : k + ROWS, at : at + LANES]
                    for a in (1, 2):
                        value = value + scales[a] * diffs[a, k : k + ROWS, at : at + LANES]
                    pieces.append(split(value))
                highs.append(jnp.concatenate([piece[0] for piece in pieces], axis=1))
                lows.append(jnp.concatenate([piece[1] for piece in pieces], axis=1))
        high, low = jnp.concatenate(highs, axis=0), jnp.concatenate(lows, axis=0)
        columns = slice(tiles[0][0], tiles[-1][0] + LANES)
        main = lax.dot_general(field[:, columns], high, dims, preferred_element_type=jnp.float32)
        rest = lax.dot_general(field[:modes, columns], low, dims, preferred_element_type=jnp.float32)
        value = main[:modes] + (main[modes:] + rest)
        sums[s, half] = value if fresh else sums[s, half] + value

    def far(s, half, z):
        return pltpu.make_async_remote_copy(
            src_ref=sums.at[s, half, z * own_j : (z + 1) * own_j, :], dst_ref=landed.at[s, half, z],
            send_sem=far_send.at[s, half, z], recv_sem=far_recv.at[s, half, z],
            device_id=(shifted(s) * 2 + core, gy), device_id_type=MESH,
        )

    def along(half, z):
        return pltpu.make_async_remote_copy(
            src_ref=line.at[z, half], dst_ref=line_in.at[gy, half],
            send_sem=line_send.at[z, half], recv_sem=line_recv.at[gy, half],
            device_id=(gx, z), device_id_type=MESH,
        )

    def along_in(half, z):
        return pltpu.make_async_remote_copy(
            src_ref=line_in.at[z, half], dst_ref=line_in.at[z, half],
            send_sem=line_send.at[z, half], recv_sem=line_recv.at[z, half],
            device_id=mate, device_id_type=MESH,
        )

    def sweep(count, body):
        def step(u, carry):
            body(u)
            return carry

        lax.fori_loop(0, count, step, 0)

    cross = chips - 1
    prepare(0, x_ref, w_ref)
    sweep(halves, lambda u: block(cross, u, first[0], True))
    for index in (0, 1):
        copies[index].wait_recv()
    prepare(1, other_x, other_w)
    sweep(halves, lambda u: block(cross, u, first[1], False))
    for index in (2, 3):
        copies[index].wait_recv()
    prepare_late(0, x_ref, w_ref)
    prepare_late(1, other_x, other_w)

    def send(s, half):
        for z in range(ny):
            far(s, half, z).start()

    def crossing(u):
        block(cross, u, late, False)
        send(cross, u)

    def straight(u):
        s, half = cross - 1 - u % (cross - 1), u // (cross - 1)
        block(s, half, first[0] + first[1] + late, True)
        send(s, half)

    def own(half):
        block(0, half, first[0] + first[1] + late, True)
        for z in range(ny):
            total = sums[0, half, z * own_j : (z + 1) * own_j, :]
            for s in range(cross, 0, -1):
                far(s, half, z).wait_recv()
                total = total + landed[s, half, z]
            line[z, half] = total

            @pl.when(gy != z)
            def _():
                along(half, z).start()

    sweep(halves, crossing)
    sweep(halves * (cross - 1), straight)
    sweep(halves, own)
    for half in range(halves):
        total = line[gy, half]
        for t in range(1, ny):
            z = (gy + t) % ny
            along_in(half, z).wait_recv()
            total = total + line_in[z, half]
        for i in range(unit):
            out_ref[half * unit + i] = total[:, i * modes : (i + 1) * modes]
    for copy in copies:
        copy.wait_send()
    for half in range(halves):
        for s in range(1, chips):
            for z in range(ny):
                far(s, half, z).wait_send()
        for t in range(1, ny):
            along(half, (gy + t) % ny).wait_send()


def per_device(modes, weights):
    mode_count, cells = modes.shape[1:]
    nx, ny = lax.axis_size("gx"), lax.axis_size("gy")
    _, _, plane, pack, unit, halves, stages = sizes(nx, ny, mode_count, cells)
    factor = 1.0 / math.sqrt(cells * nx * ny)
    rows = 3 * mode_count
    own_i, own_j = mode_count // nx, mode_count // ny
    edge = (rows // pack + 8, plane * pack)
    depth = 2 * stages * cells + 4 * plane
    wide = unit * mode_count
    vmem = pl.BlockSpec(memory_space=pltpu.VMEM)
    chips = nx // 2
    near_count = 4
    return pl.pallas_call(
        functools.partial(kernel, nx, ny, mode_count, factor),
        out_shape=jax.ShapeDtypeStruct((own_i, own_j, mode_count), jnp.float32),
        in_specs=[vmem, vmem],
        out_specs=vmem,
        scratch_shapes=[
            pltpu.VMEM((rows, cells), jnp.float32),
            pltpu.VMEM((1, cells), jnp.float32),
            pltpu.VMEM(edge, jnp.float32),
            pltpu.VMEM((2, *edge), jnp.float32),
            pltpu.VMEM((nx * halves, 3, unit, 2 * cells + 4 * plane), jnp.float32),
            pltpu.VMEM((3, mode_count, depth), jnp.float32),
            pltpu.VMEM((2 * mode_count, depth), jnp.bfloat16),
            pltpu.VMEM((chips, halves, mode_count, wide), jnp.float32),
            pltpu.VMEM((chips, halves, ny, own_j, wide), jnp.float32),
            pltpu.VMEM((ny, halves, own_j, wide), jnp.float32),
            pltpu.VMEM((ny, halves, own_j, wide), jnp.float32),
            pltpu.SemaphoreType.DMA((near_count,)),
            pltpu.SemaphoreType.DMA((near_count,)),
            pltpu.SemaphoreType.DMA((chips, halves, ny)),
            pltpu.SemaphoreType.DMA((chips, halves, ny)),
            pltpu.SemaphoreType.DMA((ny, halves)),
            pltpu.SemaphoreType.DMA((ny, halves)),
        ],
        compiler_params=pltpu.CompilerParams(collective_id=0, has_side_effects=True),
        name="tensor",
    )(modes.reshape(rows, cells), weights.reshape(1, cells))


def solution(mesh):
    return jax.shard_map(
        per_device,
        mesh=mesh,
        in_specs=(P(None, None, ("gx", "gy")), P(("gx", "gy"))),
        out_specs=P("gx", "gy", None),
        check_vma=False,
    )
```

```python
import functools
import math

import jax
import jax.numpy as jnp
from jax import lax
from jax.experimental import pallas as pl
from jax.experimental.pallas import tpu as pltpu
from jax.sharding import PartitionSpec as P

CX = 1
CY = 2
LANES = 128
ROWS = 16
UNIT = 4
FILL0 = 1
FILL = 0
MESH = pl.DeviceIdType.MESH


def partner_of(gx):
    return gx + 1 - 2 * (gx % 2)


def split(value):
    high = value.astype(jnp.bfloat16)
    low = (value - high.astype(jnp.float32)).astype(jnp.bfloat16)
    return high, low


def sizes(nx, ny, modes, cells):
    width, height = CX * nx, CY * ny
    plane = width * height
    own_i = modes // nx
    unit = UNIT if own_i % UNIT == 0 else own_i
    stages = 3 if cells > plane else 2
    return width, height, plane, max(1, LANES // plane), unit, own_i // unit, stages


def kernel(
    nx, ny, modes, factor,
    x_in, w_in, out_ref,
    x_ref, w_ref, other_x, other_w, edges, halos, weighted, diffs, field, sums, landed, line, line_in,
    load, near_send, near_recv, far_send, far_recv, line_send, line_recv,
):
    rows, cells = x_ref.shape
    width, height, plane, pack, unit, halves, stages = sizes(nx, ny, modes, cells)
    chips = nx // 2
    devices = nx * ny
    own_j = modes // ny
    early = stages * cells
    part = rows // pack
    gx, gy = lax.axis_index("gx"), lax.axis_index("gy")
    core, place = gx % 2, gx // 2
    mate = (partner_of(gx), gy)
    minor = 2 - chips % 2
    major = chips // minor

    def shifted(s):
        return (place // minor + s // minor) % major * minor + (place % minor + s % minor) % minor

    def beside(step, x, y):
        other = (x * ny + y + step + devices) % devices
        return other // ny, other % ny

    after = beside(1, gx, gy)
    after_mate = (partner_of(after[0]), after[1])
    before = beside(-1, gx, gy)
    before_mate = beside(-1, *mate)

    barrier = pltpu.get_barrier_semaphore()
    greeted = [mate, before, before_mate]
    greeted += [(shifted(s) * 2 + core, gy) for s in range(1, chips)]
    greeted += [(gx, (gy + t) % ny) for t in range(1, ny)]
    loads = [pltpu.make_async_copy(x_in, x_ref, load.at[0]), pltpu.make_async_copy(w_in, w_ref, load.at[1])]
    for copy in loads:
        copy.start()
    for device in greeted:
        pl.semaphore_signal(barrier, inc=1, device_id=device, device_id_type=MESH)
    for copy in loads:
        copy.wait()

    def turned(value, step):
        span = value.shape[1]
        shift = (-step) % span
        return pltpu.roll(value, shift, 1) if shift else value

    start = cells - plane
    if pack == 1:
        edges[:rows] = x_ref[:, start:]
        edges[rows:] = jnp.broadcast_to(w_ref[:, start:], (8, plane))
    else:
        base = start // LANES * LANES
        lane = lax.broadcasted_iota(jnp.int32, (part, LANES), 1)
        packed = jnp.zeros((part, LANES), jnp.float32)
        for p in range(pack):
            piece = turned(x_ref[p * part : (p + 1) * part, base : base + LANES], start - base - p * plane)
            packed = jnp.where(lane // plane == p, piece, packed)
        edges[:part] = packed
        edges[part:] = jnp.broadcast_to(turned(w_ref[:, base : base + LANES], start - base), (8, LANES))

    def near(index, src, dst, device):
        return pltpu.make_async_remote_copy(
            src_ref=src, dst_ref=dst, send_sem=near_send.at[index], recv_sem=near_recv.at[index],
            device_id=device, device_id_type=MESH,
        )

    copies = [
        near(0, w_in, other_w, mate),
        near(1, x_in, other_x, mate),
        near(2, edges, halos.at[0], after),
        near(3, edges, halos.at[1], after_mate),
    ]
    pl.semaphore_wait(barrier, len(greeted))
    for index in (1, 0, 2, 3):
        copies[index].start()

    span = max(plane, LANES)
    lane = lax.broadcasted_iota(jnp.int32, (modes, span), 1)
    at_x, at_y = lane % width, lane // width % height
    whole = lax.broadcasted_iota(jnp.int32, (modes, cells), 1)

    def keep(a, value, weight, scale_at, field_at):
        size = value.shape[1]
        scaled = value * weight
        for n in range(nx * halves):
            weighted[n, a, :, scale_at : scale_at + size] = scaled[n * unit : (n + 1) * unit]
        for at in field_at:
            high, low = split(value)
            field[:modes, at : at + size] = high
            field[modes:, at : at + size] = low

    def prepare(which, ref, weight_ref):
        for a in range(3):
            for c in range(0, cells, span):
                value = ref[a * modes : (a + 1) * modes, c : c + span]
                at = which * early + c
                weight = weight_ref[:, c : c + span] * factor
                keep(a, value, weight, which * cells + c, [at + a * cells] if a < stages else [])
                up = jnp.where(at_x == width - 1, turned(value, 1 - width), turned(value, 1))
                down = jnp.where(at_x == 0, turned(value, width - 1), turned(value, -1))
                diffs[a, :, at : at + span] = (up - down) * 0.5
                turn = (height - 1) * width
                up = jnp.where(at_y == height - 1, turned(value, -turn), turned(value, width))
                down = jnp.where(at_y == 0, turned(value, turn), turned(value, -width))
                diffs[a, :, at + cells : at + cells + span] = (up - down) * 0.5
            if stages == 3:
                value = ref[a * modes : (a + 1) * modes, :]
                up = jnp.where(whole < cells - plane, turned(value, plane), 0.0)
                down = jnp.where(whole >= plane, turned(value, -plane), 0.0)
                at = which * early + 2 * cells
                diffs[a, :, at : at + cells] = (up - down) * 0.5

    def prepare_late(which, ref, weight_ref):
        at, scale_at = 2 * early + which * 2 * plane, 2 * cells + which * 2 * plane
        if pack == 1:
            for a in range(3):
                mine = slice(a * modes, (a + 1) * modes)
                own, halo = ref[mine, :plane], halos[which, mine, :]
                for value, other, weight, step in (
                    (own, halo * -0.5, weight_ref[:, :plane], 0),
                    (halo, own * 0.5, halos[which, rows : rows + 1, :], plane),
                ):
                    keep(a, value, weight * factor, scale_at + step, [at + step] if a == 2 else [])
                    diffs[a, :, at + step : at + step + plane] = other
            return
        narrow = lax.broadcasted_iota(jnp.int32, (8, LANES), 1)
        low_part = narrow < plane
        weight = jnp.where(low_part[:1], weight_ref[:, :LANES], turned(halos[which, part : part + 1, :], -plane))
        for a in range(3):
            values = []
            for r in range(0, modes, 8):
                q = a * modes + r
                own = ref[q : q + 8, :LANES]
                halo = halos[which, q % part : q % part + 8, :]
                halo = turned(halo, (q // part - 1) * plane)
                values.append(jnp.where(low_part, own, halo))
                diffs[a, r : r + 8, at : at + LANES] = turned(jnp.where(low_part, own, -halo), plane) * 0.5
            keep(a, jnp.concatenate(values, axis=0), weight * factor, scale_at, [at] if a == 2 else [])

    dims = (((1,), (1,)), ((), ()))
    first = [
        [(which * early + b * cells + c, which * cells + c) for b in range(stages) for c in range(0, cells, LANES)]
        for which in range(2)
    ]
    late = [(2 * early + c, 2 * cells + c) for c in range(0, 4 * plane, LANES)]

    def block(s, half, tiles, fresh):
        group = (shifted(s) * 2 + core) * halves + half
        highs, lows = [], []
        for i in range(unit):
            for k in range(0, modes, ROWS):
                pieces = []
                for at, scale_at in tiles:
                    scales = [
                        weighted[group, a, i : i + 1, scale_at : scale_at + LANES] for a in range(3)
                    ]
                    value = scales[0] * diffs[0, k : k + ROWS, at : at + LANES]
                    for a in (1, 2):
                        value = value + scales[a] * diffs[a, k : k + ROWS, at : at + LANES]
                    pieces.append(split(value))
                highs.append(jnp.concatenate([piece[0] for piece in pieces], axis=1))
                lows.append(jnp.concatenate([piece[1] for piece in pieces], axis=1))
        high, low = jnp.concatenate(highs, axis=0), jnp.concatenate(lows, axis=0)
        columns = slice(tiles[0][0], tiles[-1][0] + LANES)
        main = lax.dot_general(field[:, columns], high, dims, preferred_element_type=jnp.float32)
        rest = lax.dot_general(field[:modes, columns], low, dims, preferred_element_type=jnp.float32)
        value = main[:modes] + (main[modes:] + rest)
        sums[s, half] = value if fresh else sums[s, half] + value

    def rank(k):
        if k == ny - 1:
            return gy
        return jnp.where(gy == 0, ny - 1 - k, k + (k - gy + ny) // ny)

    def rows_of(z):
        return pl.ds(pl.multiple_of(z * own_j, own_j), own_j)

    def far(s, half, z):
        return pltpu.make_async_remote_copy(
            src_ref=sums.at[s, half, rows_of(z), :], dst_ref=landed.at[s, half, z],
            send_sem=far_send.at[s, half, z], recv_sem=far_recv.at[s, half, z],
            device_id=(shifted(s) * 2 + core, gy), device_id_type=MESH,
        )

    def along(half, z):
        return pltpu.make_async_remote_copy(
            src_ref=line.at[z, half], dst_ref=line_in.at[gy, half],
            send_sem=line_send.at[z, half], recv_sem=line_recv.at[gy, half],
            device_id=(gx, z), device_id_type=MESH,
        )

    def along_in(half, z):
        return pltpu.make_async_remote_copy(
            src_ref=line_in.at[z, half], dst_ref=line_in.at[z, half],
            send_sem=line_send.at[z, half], recv_sem=line_recv.at[z, half],
            device_id=mate, device_id_type=MESH,
        )

    def sweep(count, body):
        def step(u, carry):
            body(u)
            return carry

        lax.fori_loop(0, count, step, 0)

    others = chips - 1
    home = -(place // minor) % major * minor + -(place % minor) % minor
    lead = home + others * (1 - (home + others) // chips)
    turn_by = 1 - 2 * (lead % 2)

    def target(k):
        return (lead - 1 + turn_by * k + others * chips) % others + 1

    def follower(u):
        return target(1 + u % (others - 1)), u // (others - 1)

    prepare(0, x_ref, w_ref)
    sweep(halves, lambda u: block(lead, u, first[0], True))
    for index in (0, 1):
        copies[index].wait_recv()
    prepare(1, other_x, other_w)
    sweep(halves, lambda u: block(lead, u, first[1], False))
    ahead = jnp.where(gy == 0, FILL0, FILL)
    sweep(ahead, lambda u: block(*follower(u), first[0] + first[1], True))
    for index in (2, 3):
        copies[index].wait_recv()
    prepare_late(0, x_ref, w_ref)
    prepare_late(1, other_x, other_w)

    def send(s, half, places):
        for k in places:
            far(s, half, rank(k)).start()

    def leading(u):
        block(lead, u, late, False)
        send(lead, u, range(1))

    def finish(u):
        s, half = follower(u)
        block(s, half, late, False)
        send(s, half, range(ny))

    def following(u):
        s, half = follower(u)
        block(s, half, first[0] + first[1] + late, True)
        send(s, half, range(ny))

    def own(half):
        block(0, half, first[0] + first[1] + late, True)

    sweep(halves, leading)
    for k in range(1, ny):
        for half in range(halves):
            send(lead, half, [k])
    sweep(ahead, finish)
    lax.fori_loop(ahead, halves * (others - 1), lambda u, carry: (following(u), carry)[1], 0)
    sweep(halves, own)
    for k in range(ny):
        z = rank(k)
        for half in range(halves):
            total = sums[0, half, rows_of(z), :]
            for s in range(others, 0, -1):
                far(s, half, z).wait_recv()
                total = total + landed[s, half, z]
            line[z, half] = total
            if k < ny - 1:
                along(half, z).start()

    for half in range(halves):
        total = line[gy, half]
        for t in range(1, ny):
            z = (gy + t) % ny
            along_in(half, z).wait_recv()
            total = total + line_in[z, half]
        for i in range(unit):
            out_ref[half * unit + i] = total[:, i * modes : (i + 1) * modes]
    for copy in copies:
        copy.wait_send()
    for half in range(halves):
        for s in range(1, chips):
            for z in range(ny):
                far(s, half, z).wait_send()
        for t in range(1, ny):
            along(half, (gy + t) % ny).wait_send()


def per_device(modes, weights):
    mode_count, cells = modes.shape[1:]
    nx, ny = lax.axis_size("gx"), lax.axis_size("gy")
    _, _, plane, pack, unit, halves, stages = sizes(nx, ny, mode_count, cells)
    factor = 1.0 / math.sqrt(cells * nx * ny)
    rows = 3 * mode_count
    own_i, own_j = mode_count // nx, mode_count // ny
    edge = (rows // pack + 8, plane * pack)
    depth = 2 * stages * cells + 4 * plane
    wide = unit * mode_count
    vmem = pl.BlockSpec(memory_space=pltpu.VMEM)
    chips = nx // 2
    near_count = 4
    return pl.pallas_call(
        functools.partial(kernel, nx, ny, mode_count, factor),
        out_shape=jax.ShapeDtypeStruct((own_i, own_j, mode_count), jnp.float32),
        in_specs=[pl.BlockSpec(memory_space=pltpu.HBM)] * 2,
        out_specs=vmem,
        scratch_shapes=[
            pltpu.VMEM((rows, cells), jnp.float32),
            pltpu.VMEM((1, cells), jnp.float32),
            pltpu.VMEM((rows, cells), jnp.float32),
            pltpu.VMEM((1, cells), jnp.float32),
            pltpu.VMEM(edge, jnp.float32),
            pltpu.VMEM((2, *edge), jnp.float32),
            pltpu.VMEM((nx * halves, 3, unit, 2 * cells + 4 * plane), jnp.float32),
            pltpu.VMEM((3, mode_count, depth), jnp.float32),
            pltpu.VMEM((2 * mode_count, depth), jnp.bfloat16),
            pltpu.VMEM((chips, halves, mode_count, wide), jnp.float32),
            pltpu.VMEM((chips, halves, ny, own_j, wide), jnp.float32),
            pltpu.VMEM((ny, halves, own_j, wide), jnp.float32),
            pltpu.VMEM((ny, halves, own_j, wide), jnp.float32),
            pltpu.SemaphoreType.DMA((2,)),
            pltpu.SemaphoreType.DMA((near_count,)),
            pltpu.SemaphoreType.DMA((near_count,)),
            pltpu.SemaphoreType.DMA((chips, halves, ny)),
            pltpu.SemaphoreType.DMA((chips, halves, ny)),
            pltpu.SemaphoreType.DMA((ny, halves)),
            pltpu.SemaphoreType.DMA((ny, halves)),
        ],
        compiler_params=pltpu.CompilerParams(collective_id=0, has_side_effects=True, vmem_limit_bytes=24 << 20),
        name="tensor",
    )(pltpu.with_memory_space_constraint(modes.reshape(rows, cells), pltpu.HBM), pltpu.with_memory_space_constraint(weights.reshape(1, cells), pltpu.HBM))


def solution(mesh):
    return jax.shard_map(
        per_device,
        mesh=mesh,
        in_specs=(P(None, None, ("gx", "gy")), P(("gx", "gy"))),
        out_specs=P("gx", "gy", None),
        check_vma=False,
    )
```

```python
import functools
import math

import jax
import jax.numpy as jnp
from jax import lax
from jax.experimental import pallas as pl
from jax.experimental.pallas import tpu as pltpu
from jax.sharding import PartitionSpec as P

CX = 1
CY = 2
LANES = 128
ROWS = 16
UNIT = 4
FILL0 = 1
FILL = 1
MESH = pl.DeviceIdType.MESH


def partner_of(gx):
    return gx + 1 - 2 * (gx % 2)


def split(value):
    high = value.astype(jnp.bfloat16)
    low = (value - high.astype(jnp.float32)).astype(jnp.bfloat16)
    return high, low


def sizes(nx, ny, modes, cells):
    width, height = CX * nx, CY * ny
    plane = width * height
    own_i = modes // nx
    unit = UNIT if own_i % UNIT == 0 else own_i
    stages = 3 if cells > plane else 2
    return width, height, plane, max(1, LANES // plane), unit, own_i // unit, stages


def kernel(
    nx, ny, modes, factor,
    x_in, w_in, out_ref,
    x_ref, w_ref, other_x, other_w, edges, halos, weighted, diffs, field, sums, landed, line, line_in,
    load, near_send, near_recv, far_send, far_recv, line_send, line_recv,
):
    rows, cells = x_ref.shape
    width, height, plane, pack, unit, halves, stages = sizes(nx, ny, modes, cells)
    chips = nx // 2
    devices = nx * ny
    own_j = modes // ny
    early = stages * cells
    part = rows // pack
    gx, gy = lax.axis_index("gx"), lax.axis_index("gy")
    core, place = gx % 2, gx // 2
    mate = (partner_of(gx), gy)
    minor = 2 - chips % 2
    major = chips // minor

    def shifted(s):
        return (place // minor + s // minor) % major * minor + (place % minor + s % minor) % minor

    def beside(step, x, y):
        other = (x * ny + y + step + devices) % devices
        return other // ny, other % ny

    after = beside(1, gx, gy)
    after_mate = (partner_of(after[0]), after[1])
    before = beside(-1, gx, gy)
    before_mate = beside(-1, *mate)

    barrier = pltpu.get_barrier_semaphore()
    greeted = [mate, before, before_mate]
    greeted += [(shifted(s) * 2 + core, gy) for s in range(1, chips)]
    greeted += [(gx, (gy + t) % ny) for t in range(1, ny)]
    loads = [pltpu.make_async_copy(x_in, x_ref, load.at[0]), pltpu.make_async_copy(w_in, w_ref, load.at[1])]
    for copy in loads:
        copy.start()
    for device in greeted:
        pl.semaphore_signal(barrier, inc=1, device_id=device, device_id_type=MESH)
    for copy in loads:
        copy.wait()

    def turned(value, step):
        span = value.shape[1]
        shift = (-step) % span
        return pltpu.roll(value, shift, 1) if shift else value

    start = cells - plane
    if pack == 1:
        edges[:rows] = x_ref[:, start:]
        edges[rows:] = jnp.broadcast_to(w_ref[:, start:], (8, plane))
    else:
        base = start // LANES * LANES
        lane = lax.broadcasted_iota(jnp.int32, (part, LANES), 1)
        packed = jnp.zeros((part, LANES), jnp.float32)
        for p in range(pack):
            piece = turned(x_ref[p * part : (p + 1) * part, base : base + LANES], start - base - p * plane)
            packed = jnp.where(lane // plane == p, piece, packed)
        edges[:part] = packed
        edges[part:] = jnp.broadcast_to(turned(w_ref[:, base : base + LANES], start - base), (8, LANES))

    def near(index, src, dst, device):
        return pltpu.make_async_remote_copy(
            src_ref=src, dst_ref=dst, send_sem=near_send.at[index], recv_sem=near_recv.at[index],
            device_id=device, device_id_type=MESH,
        )

    copies = [
        near(0, w_in, other_w, mate),
        near(1, x_in, other_x, mate),
        near(2, edges, halos.at[0], after),
        near(3, edges, halos.at[1], after_mate),
    ]
    pl.semaphore_wait(barrier, len(greeted))
    for index in (1, 0, 2, 3):
        copies[index].start()

    span = max(plane, LANES)
    lane = lax.broadcasted_iota(jnp.int32, (modes, span), 1)
    at_x, at_y = lane % width, lane // width % height
    whole = lax.broadcasted_iota(jnp.int32, (modes, cells), 1)

    def keep(a, value, weight, scale_at, field_at):
        size = value.shape[1]
        scaled = value * weight
        for n in range(nx * halves):
            weighted[n, a, :, scale_at : scale_at + size] = scaled[n * unit : (n + 1) * unit]
        for at in field_at:
            high, low = split(value)
            field[:modes, at : at + size] = high
            field[modes:, at : at + size] = low

    def across(value, at, count, step):
        turn = (count - 1) * step
        if span == LANES:
            up = jnp.take_along_axis(value, jnp.where(at == count - 1, lane - turn, lane + step), axis=1)
            down = jnp.take_along_axis(value, jnp.where(at == 0, lane + turn, lane - step), axis=1)
        else:
            up = jnp.where(at == count - 1, turned(value, -turn), turned(value, step))
            down = jnp.where(at == 0, turned(value, turn), turned(value, -step))
        return up - down

    def prepare(which, ref, weight_ref):
        for a in range(3):
            for c in range(0, cells, span):
                value = ref[a * modes : (a + 1) * modes, c : c + span]
                at = which * early + c
                weight = weight_ref[:, c : c + span] * factor
                keep(a, value, weight, which * cells + c, [at + a * cells] if a < stages else [])
                diffs[a, :, at : at + span] = across(value, at_x, width, 1)
                diffs[a, :, at + cells : at + cells + span] = across(value, at_y, height, width)
            if stages == 3:
                value = ref[a * modes : (a + 1) * modes, :]
                up = jnp.where(whole < cells - plane, turned(value, plane), 0.0)
                down = jnp.where(whole >= plane, turned(value, -plane), 0.0)
                at = which * early + 2 * cells
                diffs[a, :, at : at + cells] = up - down

    def prepare_late(which, ref, weight_ref):
        at, scale_at = 2 * early + which * 2 * plane, 2 * cells + which * 2 * plane
        if pack == 1:
            for a in range(3):
                mine = slice(a * modes, (a + 1) * modes)
                own, halo = ref[mine, :plane], halos[which, mine, :]
                for value, other, weight, step in (
                    (own, -halo, weight_ref[:, :plane], 0),
                    (halo, own, halos[which, rows : rows + 1, :], plane),
                ):
                    keep(a, value, weight * factor, scale_at + step, [at + step] if a == 2 else [])
                    diffs[a, :, at + step : at + step + plane] = other
            return
        narrow = lax.broadcasted_iota(jnp.int32, (8, LANES), 1)
        low_part = narrow < plane
        weight = jnp.where(low_part[:1], weight_ref[:, :LANES], turned(halos[which, part : part + 1, :], -plane))
        for a in range(3):
            values = []
            for r in range(0, modes, 8):
                q = a * modes + r
                own = ref[q : q + 8, :LANES]
                halo = halos[which, q % part : q % part + 8, :]
                halo = turned(halo, (q // part - 1) * plane)
                values.append(jnp.where(low_part, own, halo))
                diffs[a, r : r + 8, at : at + LANES] = turned(jnp.where(low_part, own, -halo), plane)
            keep(a, jnp.concatenate(values, axis=0), weight * factor, scale_at, [at] if a == 2 else [])

    dims = (((1,), (1,)), ((), ()))
    first = [
        [(which * early + b * cells + c, which * cells + c) for b in range(stages) for c in range(0, cells, LANES)]
        for which in range(2)
    ]
    late = [(2 * early + c, 2 * cells + c) for c in range(0, 4 * plane, LANES)]

    def block(s, half, tiles, fresh):
        group = (shifted(s) * 2 + core) * halves + half
        highs, lows = [], []
        for i in range(unit):
            for k in range(0, modes, ROWS):
                pieces = []
                for at, scale_at in tiles:
                    scales = [
                        weighted[group, a, i : i + 1, scale_at : scale_at + LANES] for a in range(3)
                    ]
                    value = scales[0] * diffs[0, k : k + ROWS, at : at + LANES]
                    for a in (1, 2):
                        value = value + scales[a] * diffs[a, k : k + ROWS, at : at + LANES]
                    pieces.append(split(value))
                highs.append(jnp.concatenate([piece[0] for piece in pieces], axis=1))
                lows.append(jnp.concatenate([piece[1] for piece in pieces], axis=1))
        high, low = jnp.concatenate(highs, axis=0), jnp.concatenate(lows, axis=0)
        columns = slice(tiles[0][0], tiles[-1][0] + LANES)
        main = lax.dot_general(field[:, columns], high, dims, preferred_element_type=jnp.float32)
        rest = lax.dot_general(field[:modes, columns], low, dims, preferred_element_type=jnp.float32)
        value = main[:modes] + (main[modes:] + rest)
        sums[s, half] = value if fresh else sums[s, half] + value

    def rank(k):
        if k == ny - 1:
            return gy
        return jnp.where(gy == 0, ny - 1 - k, k + (k - gy + ny) // ny)

    def rows_of(z):
        return pl.ds(pl.multiple_of(z * own_j, own_j), own_j)

    def far(s, half, z):
        return pltpu.make_async_remote_copy(
            src_ref=sums.at[s, half, rows_of(z), :], dst_ref=landed.at[half, z, s - 1],
            send_sem=far_send.at[0], recv_sem=far_recv.at[half, z],
            device_id=(shifted(s) * 2 + core, gy), device_id_type=MESH,
        )

    def along(half, z):
        slot = (gy - z + ny) % ny - 1
        return pltpu.make_async_remote_copy(
            src_ref=line.at[half, z], dst_ref=line_in.at[slot, half],
            send_sem=line_send.at[0], recv_sem=line_recv.at[0],
            device_id=(gx, z), device_id_type=MESH,
        )

    def all_of(ref, send_sem, recv_sem):
        return pltpu.make_async_remote_copy(
            src_ref=ref, dst_ref=ref, send_sem=send_sem, recv_sem=recv_sem,
            device_id=mate, device_id_type=MESH,
        )

    def sweep(count, body):
        def step(u, carry):
            body(u)
            return carry

        lax.fori_loop(0, count, step, 0)

    others = chips - 1
    home = -(place // minor) % major * minor + -(place % minor) % minor
    lead = home + others * (1 - (home + others) // chips)
    turn_by = 1 - 2 * (lead % 2)

    def target(k):
        return (lead - 1 + turn_by * k + others * chips) % others + 1

    def follower(u):
        return target(1 + u % (others - 1)), u // (others - 1)

    prepare(0, x_ref, w_ref)
    for half in range(halves):
        block(lead, half, first[0], True)
    for index in (0, 1):
        copies[index].wait_recv()
    prepare(1, other_x, other_w)
    for half in range(halves):
        block(lead, half, first[1], False)
    ahead = jnp.where(gy == 0, FILL0, FILL)
    sweep(ahead, lambda u: block(*follower(u), first[0] + first[1], True))
    for index in (2, 3):
        copies[index].wait_recv()
    prepare_late(0, x_ref, w_ref)
    prepare_late(1, other_x, other_w)

    def send(s, half, places):
        for k in places:
            far(s, half, rank(k)).start()

    def leading(u):
        block(lead, u, late, False)
        send(lead, u, range(1))

    def finish(u):
        s, half = follower(u)
        block(s, half, late, False)
        send(s, half, range(ny))

    def following(u):
        s, half = follower(u)
        block(s, half, first[0] + first[1] + late, True)
        send(s, half, range(ny))

    def own(half):
        block(0, half, first[0] + first[1] + late, True)

    for half in range(halves):
        leading(half)
    for k in range(1, ny):
        for half in range(halves):
            send(lead, half, [k])
    sweep(ahead, finish)
    lax.fori_loop(ahead, halves * (others - 1), lambda u, carry: (following(u), carry)[1], 0)
    sweep(halves, own)
    for k in range(ny):
        z = rank(k)
        for half in range(halves):
            all_of(landed.at[half, z], far_send.at[0], far_recv.at[half, z]).wait_recv()
            total = sums[0, half, rows_of(z), :]
            for s in range(others):
                total = total + landed[half, z, s]
            line[half, z] = total
            if k < ny - 1:
                along(half, z).start()
    for copy in copies:
        copy.wait_send()
    all_of(sums.at[1:], far_send.at[0], far_recv.at[0, 0]).wait_send()
    arrived = all_of(line_in, line_send.at[0], line_recv.at[0])
    arrived.wait_recv()
    for half in range(halves):
        total = line[half, gy]
        for t in range(ny - 1):
            total = total + line_in[t, half]
        for i in range(unit):
            out_ref[half * unit + i] = total[:, i * modes : (i + 1) * modes]
    arrived.wait_send()


def per_device(modes, weights):
    mode_count, cells = modes.shape[1:]
    nx, ny = lax.axis_size("gx"), lax.axis_size("gy")
    _, _, plane, pack, unit, halves, stages = sizes(nx, ny, mode_count, cells)
    factor = 0.5 / math.sqrt(cells * nx * ny)
    rows = 3 * mode_count
    own_i, own_j = mode_count // nx, mode_count // ny
    edge = (rows // pack + 8, plane * pack)
    depth = 2 * stages * cells + 4 * plane
    wide = unit * mode_count
    vmem = pl.BlockSpec(memory_space=pltpu.VMEM)
    chips = nx // 2
    near_count = 4
    return pl.pallas_call(
        functools.partial(kernel, nx, ny, mode_count, factor),
        out_shape=jax.ShapeDtypeStruct((own_i, own_j, mode_count), jnp.float32),
        in_specs=[pl.BlockSpec(memory_space=pltpu.HBM)] * 2,
        out_specs=vmem,
        scratch_shapes=[
            pltpu.VMEM((rows, cells), jnp.float32),
            pltpu.VMEM((1, cells), jnp.float32),
            pltpu.VMEM((rows, cells), jnp.float32),
            pltpu.VMEM((1, cells), jnp.float32),
            pltpu.VMEM(edge, jnp.float32),
            pltpu.VMEM((2, *edge), jnp.float32),
            pltpu.VMEM((nx * halves, 3, unit, 2 * cells + 4 * plane), jnp.float32),
            pltpu.VMEM((3, mode_count, depth), jnp.float32),
            pltpu.VMEM((2 * mode_count, depth), jnp.bfloat16),
            pltpu.VMEM((chips, halves, mode_count, wide), jnp.float32),
            pltpu.VMEM((halves, ny, chips - 1, own_j, wide), jnp.float32),
            pltpu.VMEM((halves, ny, own_j, wide), jnp.float32),
            pltpu.VMEM((ny - 1, halves, own_j, wide), jnp.float32),
            pltpu.SemaphoreType.DMA((2,)),
            pltpu.SemaphoreType.DMA((near_count,)),
            pltpu.SemaphoreType.DMA((near_count,)),
            pltpu.SemaphoreType.DMA((1,)),
            pltpu.SemaphoreType.DMA((halves, ny)),
            pltpu.SemaphoreType.DMA((1,)),
            pltpu.SemaphoreType.DMA((1,)),
        ],
        compiler_params=pltpu.CompilerParams(collective_id=0, has_side_effects=True, vmem_limit_bytes=24 << 20),
        name="tensor",
    )(pltpu.with_memory_space_constraint(modes.reshape(rows, cells), pltpu.HBM), pltpu.with_memory_space_constraint(weights.reshape(1, cells), pltpu.HBM))


def solution(mesh):
    return jax.shard_map(
        per_device,
        mesh=mesh,
        in_specs=(P(None, None, ("gx", "gy")), P(("gx", "gy"))),
        out_specs=P("gx", "gy", None),
        check_vma=False,
    )
```

```python
import functools
import math

import jax
import jax.numpy as jnp
from jax import lax
from jax.experimental import pallas as pl
from jax.experimental.pallas import tpu as pltpu
from jax.sharding import PartitionSpec as P

CX = 1
CY = 2
LANES = 128
ROWS = 16
UNIT = 4
FILL0 = 2
FILL = 1
MESH = pl.DeviceIdType.MESH


def partner_of(gx):
    return gx + 1 - 2 * (gx % 2)


def split(value):
    high = value.astype(jnp.bfloat16)
    low = (value - high.astype(jnp.float32)).astype(jnp.bfloat16)
    return high, low


def sizes(nx, ny, modes, cells):
    width, height = CX * nx, CY * ny
    plane = width * height
    own_i = modes // nx
    unit = UNIT if own_i % UNIT == 0 else own_i
    stages = 3 if cells > plane else 2
    return width, height, plane, max(1, LANES // plane), unit, own_i // unit, stages


def kernel(
    nx, ny, modes, factor,
    x_in, w_in, out_ref,
    x_ref, w_ref, other_x, other_w, edges, halos, weighted, diffs, field, sums, landed, line, line_in,
    load, near_send, near_recv, far_send, far_recv, line_send, line_recv,
):
    rows, cells = x_ref.shape
    width, height, plane, pack, unit, halves, stages = sizes(nx, ny, modes, cells)
    chips = nx // 2
    devices = nx * ny
    own_j = modes // ny
    early = stages * cells
    part = rows // pack
    gx, gy = lax.axis_index("gx"), lax.axis_index("gy")
    core, place = gx % 2, gx // 2
    mate = (partner_of(gx), gy)
    minor = 2 - chips % 2
    major = chips // minor

    def shifted(s):
        return (place // minor + s // minor) % major * minor + (place % minor + s % minor) % minor

    def beside(step, x, y):
        other = (x * ny + y + step + devices) % devices
        return other // ny, other % ny

    after = beside(1, gx, gy)
    after_mate = (partner_of(after[0]), after[1])
    before = beside(-1, gx, gy)
    before_mate = beside(-1, *mate)

    barrier = pltpu.get_barrier_semaphore()
    greeted = [mate, before, before_mate]
    greeted += [(shifted(s) * 2 + core, gy) for s in range(1, chips)]
    greeted += [(gx, (gy + t) % ny) for t in range(1, ny)]
    loads = [pltpu.make_async_copy(x_in, x_ref, load.at[0]), pltpu.make_async_copy(w_in, w_ref, load.at[1])]
    for copy in loads:
        copy.start()
    for device in greeted:
        pl.semaphore_signal(barrier, inc=1, device_id=device, device_id_type=MESH)
    for copy in loads:
        copy.wait()

    def turned(value, step):
        span = value.shape[1]
        shift = (-step) % span
        return pltpu.roll(value, shift, 1) if shift else value

    start = cells - plane
    if pack == 1:
        edges[:rows] = x_ref[:, start:]
        edges[rows:] = jnp.broadcast_to(w_ref[:, start:], (8, plane))
    else:
        base = start // LANES * LANES
        lane = lax.broadcasted_iota(jnp.int32, (part, LANES), 1)
        packed = jnp.zeros((part, LANES), jnp.float32)
        for p in range(pack):
            piece = turned(x_ref[p * part : (p + 1) * part, base : base + LANES], start - base - p * plane)
            packed = jnp.where(lane // plane == p, piece, packed)
        edges[:part] = packed
        edges[part:] = jnp.broadcast_to(turned(w_ref[:, base : base + LANES], start - base), (8, LANES))

    def near(index, src, dst, device):
        return pltpu.make_async_remote_copy(
            src_ref=src, dst_ref=dst, send_sem=near_send.at[index], recv_sem=near_recv.at[index],
            device_id=device, device_id_type=MESH,
        )

    copies = [
        near(0, w_in, other_w, mate),
        near(1, x_in, other_x, mate),
        near(2, edges, halos.at[0], after),
        near(3, edges, halos.at[1], after_mate),
    ]
    def enter():
        pl.semaphore_wait(barrier, len(greeted))
        for index in (1, 0, 2, 3):
            copies[index].start()

    early_start = 1 - (place + chips - 1) // chips * ((gy + ny - 1) // ny)

    @pl.when(early_start == 0)
    def _():
        enter()


    span = max(plane, LANES)
    lane = lax.broadcasted_iota(jnp.int32, (modes, span), 1)
    at_x, at_y = lane % width, lane // width % height
    whole = lax.broadcasted_iota(jnp.int32, (modes, cells), 1)

    def keep(a, value, weight, scale_at, field_at):
        size = value.shape[1]
        scaled = value * weight
        for n in range(nx * halves):
            weighted[n, a, :, scale_at : scale_at + size] = scaled[n * unit : (n + 1) * unit]
        for at in field_at:
            high, low = split(value)
            field[:modes, at : at + size] = high
            field[modes:, at : at + size] = low

    def across(value, at, count, step):
        turn = (count - 1) * step
        if span == LANES:
            up = jnp.take_along_axis(value, jnp.where(at == count - 1, lane - turn, lane + step), axis=1)
            down = jnp.take_along_axis(value, jnp.where(at == 0, lane + turn, lane - step), axis=1)
        else:
            up = jnp.where(at == count - 1, turned(value, -turn), turned(value, step))
            down = jnp.where(at == 0, turned(value, turn), turned(value, -step))
        return up - down

    def prepare(which, ref, weight_ref):
        for a in range(3):
            for c in range(0, cells, span):
                value = ref[a * modes : (a + 1) * modes, c : c + span]
                at = which * early + c
                weight = weight_ref[:, c : c + span] * factor
                keep(a, value, weight, which * cells + c, [at + a * cells] if a < stages else [])
                diffs[a, :, at : at + span] = across(value, at_x, width, 1)
                diffs[a, :, at + cells : at + cells + span] = across(value, at_y, height, width)
            if stages == 3:
                value = ref[a * modes : (a + 1) * modes, :]
                up = jnp.where(whole < cells - plane, turned(value, plane), 0.0)
                down = jnp.where(whole >= plane, turned(value, -plane), 0.0)
                at = which * early + 2 * cells
                diffs[a, :, at : at + cells] = up - down

    def prepare_late(which, ref, weight_ref):
        at, scale_at = 2 * early + which * 2 * plane, 2 * cells + which * 2 * plane
        if pack == 1:
            for a in range(3):
                mine = slice(a * modes, (a + 1) * modes)
                own, halo = ref[mine, :plane], halos[which, mine, :]
                for value, other, weight, step in (
                    (own, -halo, weight_ref[:, :plane], 0),
                    (halo, own, halos[which, rows : rows + 1, :], plane),
                ):
                    keep(a, value, weight * factor, scale_at + step, [at + step] if a == 2 else [])
                    diffs[a, :, at + step : at + step + plane] = other
            return
        narrow = lax.broadcasted_iota(jnp.int32, (8, LANES), 1)
        low_part = narrow < plane
        weight = jnp.where(low_part[:1], weight_ref[:, :LANES], turned(halos[which, part : part + 1, :], -plane))
        for a in range(3):
            values = []
            for r in range(0, modes, 8):
                q = a * modes + r
                own = ref[q : q + 8, :LANES]
                halo = halos[which, q % part : q % part + 8, :]
                halo = turned(halo, (q // part - 1) * plane)
                values.append(jnp.where(low_part, own, halo))
                diffs[a, r : r + 8, at : at + LANES] = turned(jnp.where(low_part, own, -halo), plane)
            keep(a, jnp.concatenate(values, axis=0), weight * factor, scale_at, [at] if a == 2 else [])

    dims = (((1,), (1,)), ((), ()))
    first = [
        [(which * early + b * cells + c, which * cells + c) for b in range(stages) for c in range(0, cells, LANES)]
        for which in range(2)
    ]
    late = [(2 * early + c, 2 * cells + c) for c in range(0, 4 * plane, LANES)]

    def block(s, half, tiles, fresh):
        group = (shifted(s) * 2 + core) * halves + half
        highs, lows = [], []
        for i in range(unit):
            for k in range(0, modes, ROWS):
                pieces = []
                for at, scale_at in tiles:
                    scales = [
                        weighted[group, a, i : i + 1, scale_at : scale_at + LANES] for a in range(3)
                    ]
                    value = scales[0] * diffs[0, k : k + ROWS, at : at + LANES]
                    for a in (1, 2):
                        value = value + scales[a] * diffs[a, k : k + ROWS, at : at + LANES]
                    pieces.append(split(value))
                highs.append(jnp.concatenate([piece[0] for piece in pieces], axis=1))
                lows.append(jnp.concatenate([piece[1] for piece in pieces], axis=1))
        high, low = jnp.concatenate(highs, axis=0), jnp.concatenate(lows, axis=0)
        columns = slice(tiles[0][0], tiles[-1][0] + LANES)
        main = lax.dot_general(field[:, columns], high, dims, preferred_element_type=jnp.float32)
        rest = lax.dot_general(field[:modes, columns], low, dims, preferred_element_type=jnp.float32)
        value = main[:modes] + (main[modes:] + rest)
        sums[s, half] = value if fresh else sums[s, half] + value

    def rank(k):
        if k == ny - 1:
            return gy
        return k + (k - gy + ny) // ny

    def rows_of(z):
        return pl.ds(pl.multiple_of(z * own_j, own_j), own_j)

    def far(s, half, z):
        return pltpu.make_async_remote_copy(
            src_ref=sums.at[s, half, rows_of(z), :], dst_ref=landed.at[half, z, s - 1],
            send_sem=far_send.at[0], recv_sem=far_recv.at[half, z],
            device_id=(shifted(s) * 2 + core, gy), device_id_type=MESH,
        )

    def along(half, z):
        slot = (gy - z + ny) % ny - 1
        return pltpu.make_async_remote_copy(
            src_ref=line.at[half, z], dst_ref=line_in.at[slot, half],
            send_sem=line_send.at[0], recv_sem=line_recv.at[0],
            device_id=(gx, z), device_id_type=MESH,
        )

    def all_of(ref, send_sem, recv_sem):
        return pltpu.make_async_remote_copy(
            src_ref=ref, dst_ref=ref, send_sem=send_sem, recv_sem=recv_sem,
            device_id=mate, device_id_type=MESH,
        )

    def sweep(count, body):
        def step(u, carry):
            body(u)
            return carry

        lax.fori_loop(0, count, step, 0)

    others = chips - 1
    home = -(place // minor) % major * minor + -(place % minor) % minor
    lead = home + others * (1 - (home + others) // chips)
    turn_by = 1 - 2 * (lead % 2)

    def target(k):
        return (lead - 1 + turn_by * k + others * chips) % others + 1

    def follower(u):
        return target(1 + u // halves), u % halves

    prepare(0, x_ref, w_ref)
    for half in range(halves):
        block(lead, half, first[0], True)

    @pl.when(early_start > 0)
    def _():
        enter()

    for index in (0, 1):
        copies[index].wait_recv()
    prepare(1, other_x, other_w)
    for half in range(halves):
        block(lead, half, first[1], False)
    ahead = jnp.where(gy == 0, FILL0, FILL)
    sweep(ahead, lambda u: block(*follower(u), first[0] + first[1], True))
    for index in (2, 3):
        copies[index].wait_recv()
    prepare_late(0, x_ref, w_ref)
    prepare_late(1, other_x, other_w)

    def send(s, half, places):
        for k in places:
            far(s, half, rank(k)).start()

    def leading(u):
        block(lead, u, late, False)
        send(lead, u, range(1))

    def finish(u):
        s, half = follower(u)
        block(s, half, late, False)
        send(s, half, range(ny - 1))

    def following(u):
        s, half = follower(u)
        block(s, half, first[0] + first[1] + late, True)
        send(s, half, range(ny - 1))

    def own(half):
        block(0, half, first[0] + first[1] + late, True)

    for half in range(halves):
        block(lead, half, late, False)
    for k in range(ny - 1):
        for half in range(halves):
            send(lead, half, [k])
    sweep(ahead, finish)
    lax.fori_loop(ahead, halves * (others - 1), lambda u, carry: (following(u), carry)[1], 0)
    for half in range(halves):
        send(lead, half, [ny - 1])
    sweep(halves * (others - 1), lambda u: send(*follower(u), [ny - 1]))
    sweep(halves, own)
    for k in range(ny):
        z = rank(k)
        for half in range(halves):
            all_of(landed.at[half, z], far_send.at[0], far_recv.at[half, z]).wait_recv()
            total = sums[0, half, rows_of(z), :]
            for s in range(others):
                total = total + landed[half, z, s]
            line[half, z] = total
            if k < ny - 1:
                along(half, z).start()
    for copy in copies:
        copy.wait_send()
    all_of(sums.at[1:], far_send.at[0], far_recv.at[0, 0]).wait_send()
    arrived = all_of(line_in, line_send.at[0], line_recv.at[0])
    arrived.wait_recv()
    for half in range(halves):
        total = line[half, gy]
        for t in range(ny - 1):
            total = total + line_in[t, half]
        for i in range(unit):
            out_ref[half * unit + i] = total[:, i * modes : (i + 1) * modes]
    arrived.wait_send()


def per_device(modes, weights):
    mode_count, cells = modes.shape[1:]
    nx, ny = lax.axis_size("gx"), lax.axis_size("gy")
    _, _, plane, pack, unit, halves, stages = sizes(nx, ny, mode_count, cells)
    factor = 0.5 / math.sqrt(cells * nx * ny)
    rows = 3 * mode_count
    own_i, own_j = mode_count // nx, mode_count // ny
    edge = (rows // pack + 8, plane * pack)
    depth = 2 * stages * cells + 4 * plane
    wide = unit * mode_count
    vmem = pl.BlockSpec(memory_space=pltpu.VMEM)
    chips = nx // 2
    near_count = 4
    return pl.pallas_call(
        functools.partial(kernel, nx, ny, mode_count, factor),
        out_shape=jax.ShapeDtypeStruct((own_i, own_j, mode_count), jnp.float32),
        in_specs=[pl.BlockSpec(memory_space=pltpu.HBM)] * 2,
        out_specs=vmem,
        scratch_shapes=[
            pltpu.VMEM((rows, cells), jnp.float32),
            pltpu.VMEM((1, cells), jnp.float32),
            pltpu.VMEM((rows, cells), jnp.float32),
            pltpu.VMEM((1, cells), jnp.float32),
            pltpu.VMEM(edge, jnp.float32),
            pltpu.VMEM((2, *edge), jnp.float32),
            pltpu.VMEM((nx * halves, 3, unit, 2 * cells + 4 * plane), jnp.float32),
            pltpu.VMEM((3, mode_count, depth), jnp.float32),
            pltpu.VMEM((2 * mode_count, depth), jnp.bfloat16),
            pltpu.VMEM((chips, halves, mode_count, wide), jnp.float32),
            pltpu.VMEM((halves, ny, chips - 1, own_j, wide), jnp.float32),
            pltpu.VMEM((halves, ny, own_j, wide), jnp.float32),
            pltpu.VMEM((ny - 1, halves, own_j, wide), jnp.float32),
            pltpu.SemaphoreType.DMA((2,)),
            pltpu.SemaphoreType.DMA((near_count,)),
            pltpu.SemaphoreType.DMA((near_count,)),
            pltpu.SemaphoreType.DMA((1,)),
            pltpu.SemaphoreType.DMA((halves, ny)),
            pltpu.SemaphoreType.DMA((1,)),
            pltpu.SemaphoreType.DMA((1,)),
        ],
        compiler_params=pltpu.CompilerParams(collective_id=0, has_side_effects=True, vmem_limit_bytes=24 << 20),
        name="tensor",
    )(pltpu.with_memory_space_constraint(modes.reshape(rows, cells), pltpu.HBM), pltpu.with_memory_space_constraint(weights.reshape(1, cells), pltpu.HBM))


def solution(mesh):
    return jax.shard_map(
        per_device,
        mesh=mesh,
        in_specs=(P(None, None, ("gx", "gy")), P(("gx", "gy"))),
        out_specs=P("gx", "gy", None),
        check_vma=False,
    )
```

```python
import functools
import math

import jax
import jax.numpy as jnp
from jax import lax
from jax.experimental import pallas as pl
from jax.experimental.pallas import tpu as pltpu
from jax.sharding import PartitionSpec as P

CX = 1
CY = 2
LANES = 128
ROWS = 16
UNIT = 4
FILL0 = 2
FILL = 1
MESH = pl.DeviceIdType.MESH


def partner_of(gx):
    return gx + 1 - 2 * (gx % 2)


def split(value):
    high = value.astype(jnp.bfloat16)
    low = (value - high.astype(jnp.float32)).astype(jnp.bfloat16)
    return high, low


def sizes(nx, ny, modes, cells):
    width, height = CX * nx, CY * ny
    plane = width * height
    own_i = modes // nx
    unit = UNIT if own_i % UNIT == 0 else own_i
    stages = 3 if cells > plane else 2
    return width, height, plane, max(1, LANES // plane), unit, own_i // unit, stages


def kernel(
    nx, ny, modes, factor,
    x_in, w_in, out_ref,
    x_ref, w_ref, other_x, other_w, edges, halos, weighted, diffs, field, sums, landed, line, line_in,
    joined, load, near_send, near_recv, far_send, far_recv, line_send, line_recv,
):
    rows, cells = x_ref.shape
    width, height, plane, pack, unit, halves, stages = sizes(nx, ny, modes, cells)
    chips = nx // 2
    devices = nx * ny
    own_j = modes // ny
    early = stages * cells
    part = rows // pack
    gx, gy = lax.axis_index("gx"), lax.axis_index("gy")
    core, place = gx % 2, gx // 2
    mate = (partner_of(gx), gy)
    minor = 2 - chips % 2
    major = chips // minor

    def shifted(s):
        return (place // minor + s // minor) % major * minor + (place % minor + s % minor) % minor

    def beside(step, x, y):
        other = (x * ny + y + step + devices) % devices
        return other // ny, other % ny

    after = beside(1, gx, gy)
    after_mate = (partner_of(after[0]), after[1])
    before = beside(-1, gx, gy)
    before_mate = beside(-1, *mate)

    barrier = pltpu.get_barrier_semaphore()
    loads = [pltpu.make_async_copy(x_in, x_ref, load.at[0]), pltpu.make_async_copy(w_in, w_ref, load.at[1])]
    for copy in loads:
        copy.start()
    for device in (mate, before, before_mate):
        pl.semaphore_signal(barrier, inc=1, device_id=device, device_id_type=MESH)

    def greet(semaphore, sign):
        for q in range(chips):

            @pl.when((q - place) * sign > 0)
            def _():
                pl.semaphore_signal(semaphore[0], inc=1, device_id=(q * 2 + core, gy), device_id_type=MESH)

        for z in range(ny):

            @pl.when((z - gy) * sign > 0)
            def _():
                pl.semaphore_signal(semaphore[1], inc=1, device_id=(gx, z), device_id_type=MESH)

    greet((barrier, barrier), 1)
    for copy in loads:
        copy.wait()

    def turned(value, step):
        span = value.shape[1]
        shift = (-step) % span
        return pltpu.roll(value, shift, 1) if shift else value

    start = cells - plane
    if pack == 1:
        edges[:rows] = x_ref[:, start:]
        edges[rows:] = jnp.broadcast_to(w_ref[:, start:], (8, plane))
    else:
        base = start // LANES * LANES
        lane = lax.broadcasted_iota(jnp.int32, (part, LANES), 1)
        packed = jnp.zeros((part, LANES), jnp.float32)
        for p in range(pack):
            piece = turned(x_ref[p * part : (p + 1) * part, base : base + LANES], start - base - p * plane)
            packed = jnp.where(lane // plane == p, piece, packed)
        edges[:part] = packed
        edges[part:] = jnp.broadcast_to(turned(w_ref[:, base : base + LANES], start - base), (8, LANES))

    def near(index, src, dst, device):
        return pltpu.make_async_remote_copy(
            src_ref=src, dst_ref=dst, send_sem=near_send.at[index], recv_sem=near_recv.at[index],
            device_id=device, device_id_type=MESH,
        )

    copies = [
        near(0, w_in, other_w, mate),
        near(1, x_in, other_x, mate),
        near(2, edges, halos.at[0], after),
        near(3, edges, halos.at[1], after_mate),
    ]
    def enter():
        pl.semaphore_wait(barrier, 3 + place + gy)
        for index in (2, 3, 1, 0):
            copies[index].start()
        greet((joined.at[0], joined.at[1]), -1)

    early_start = 1 - (gy + ny - 1) // ny

    @pl.when(early_start == 0)
    def _():
        enter()


    span = max(plane, LANES)
    lane = lax.broadcasted_iota(jnp.int32, (modes, span), 1)
    at_x, at_y = lane % width, lane // width % height
    whole = lax.broadcasted_iota(jnp.int32, (modes, cells), 1)

    def keep(a, value, weight, scale_at, field_at):
        size = value.shape[1]
        scaled = value * weight
        for n in range(nx * halves):
            weighted[n, a, :, scale_at : scale_at + size] = scaled[n * unit : (n + 1) * unit]
        for at in field_at:
            high, low = split(value)
            field[:modes, at : at + size] = high
            field[modes:, at : at + size] = low

    def across(value, at, count, step):
        turn = (count - 1) * step
        if span == LANES:
            up = jnp.take_along_axis(value, jnp.where(at == count - 1, lane - turn, lane + step), axis=1)
            down = jnp.take_along_axis(value, jnp.where(at == 0, lane + turn, lane - step), axis=1)
        else:
            up = jnp.where(at == count - 1, turned(value, -turn), turned(value, step))
            down = jnp.where(at == 0, turned(value, turn), turned(value, -step))
        return up - down

    def prepare(which, ref, weight_ref):
        for a in range(3):
            for c in range(0, cells, span):
                value = ref[a * modes : (a + 1) * modes, c : c + span]
                at = which * early + c
                weight = weight_ref[:, c : c + span] * factor
                keep(a, value, weight, which * cells + c, [at + a * cells] if a < stages else [])
                diffs[a, :, at : at + span] = across(value, at_x, width, 1)
                diffs[a, :, at + cells : at + cells + span] = across(value, at_y, height, width)
            if stages == 3:
                value = ref[a * modes : (a + 1) * modes, :]
                up = jnp.where(whole < cells - plane, turned(value, plane), 0.0)
                down = jnp.where(whole >= plane, turned(value, -plane), 0.0)
                at = which * early + 2 * cells
                diffs[a, :, at : at + cells] = up - down

    def prepare_late(which, ref, weight_ref):
        at, scale_at = 2 * early + which * 2 * plane, 2 * cells + which * 2 * plane
        if pack == 1:
            for a in range(3):
                mine = slice(a * modes, (a + 1) * modes)
                own, halo = ref[mine, :plane], halos[which, mine, :]
                for value, other, weight, step in (
                    (own, -halo, weight_ref[:, :plane], 0),
                    (halo, own, halos[which, rows : rows + 1, :], plane),
                ):
                    keep(a, value, weight * factor, scale_at + step, [at + step] if a == 2 else [])
                    diffs[a, :, at + step : at + step + plane] = other
            return
        narrow = lax.broadcasted_iota(jnp.int32, (8, LANES), 1)
        low_part = narrow < plane
        weight = jnp.where(low_part[:1], weight_ref[:, :LANES], turned(halos[which, part : part + 1, :], -plane))
        for a in range(3):
            values = []
            for r in range(0, modes, 8):
                q = a * modes + r
                own = ref[q : q + 8, :LANES]
                halo = halos[which, q % part : q % part + 8, :]
                halo = turned(halo, (q // part - 1) * plane)
                values.append(jnp.where(low_part, own, halo))
                diffs[a, r : r + 8, at : at + LANES] = turned(jnp.where(low_part, own, -halo), plane)
            keep(a, jnp.concatenate(values, axis=0), weight * factor, scale_at, [at] if a == 2 else [])

    dims = (((1,), (1,)), ((), ()))
    first = [
        [(which * early + b * cells + c, which * cells + c) for b in range(stages) for c in range(0, cells, LANES)]
        for which in range(2)
    ]
    late = [(2 * early + c, 2 * cells + c) for c in range(0, 4 * plane, LANES)]

    def block(s, half, tiles, fresh):
        group = (shifted(s) * 2 + core) * halves + half
        highs, lows = [], []
        for i in range(unit):
            for k in range(0, modes, ROWS):
                pieces = []
                for at, scale_at in tiles:
                    scales = [
                        weighted[group, a, i : i + 1, scale_at : scale_at + LANES] for a in range(3)
                    ]
                    value = scales[0] * diffs[0, k : k + ROWS, at : at + LANES]
                    for a in (1, 2):
                        value = value + scales[a] * diffs[a, k : k + ROWS, at : at + LANES]
                    pieces.append(split(value))
                highs.append(jnp.concatenate([piece[0] for piece in pieces], axis=1))
                lows.append(jnp.concatenate([piece[1] for piece in pieces], axis=1))
        high, low = jnp.concatenate(highs, axis=0), jnp.concatenate(lows, axis=0)
        columns = slice(tiles[0][0], tiles[-1][0] + LANES)
        main = lax.dot_general(field[:, columns], high, dims, preferred_element_type=jnp.float32)
        rest = lax.dot_general(field[:modes, columns], low, dims, preferred_element_type=jnp.float32)
        value = main[:modes] + (main[modes:] + rest)
        sums[s, half] = value if fresh else sums[s, half] + value

    def rank(k):
        if k == ny - 1:
            return gy
        return k + (k - gy + ny) // ny

    def rows_of(z):
        return pl.ds(pl.multiple_of(z * own_j, own_j), own_j)

    def far(s, half, z):
        return pltpu.make_async_remote_copy(
            src_ref=sums.at[s, half, rows_of(z), :], dst_ref=landed.at[half, z, s - 1],
            send_sem=far_send.at[0], recv_sem=far_recv.at[half, z],
            device_id=(shifted(s) * 2 + core, gy), device_id_type=MESH,
        )

    def along(half, z):
        slot = (gy - z + ny) % ny - 1
        return pltpu.make_async_remote_copy(
            src_ref=line.at[half, z], dst_ref=line_in.at[slot, half],
            send_sem=line_send.at[0], recv_sem=line_recv.at[0],
            device_id=(gx, z), device_id_type=MESH,
        )

    def all_of(ref, send_sem, recv_sem):
        return pltpu.make_async_remote_copy(
            src_ref=ref, dst_ref=ref, send_sem=send_sem, recv_sem=recv_sem,
            device_id=mate, device_id_type=MESH,
        )

    def sweep(count, body):
        def step(u, carry):
            body(u)
            return carry

        lax.fori_loop(0, count, step, 0)

    others = chips - 1
    home = -(place // minor) % major * minor + -(place % minor) % minor
    lead = home + others * (1 - (home + others) // chips)
    turn_by = 1 - 2 * (lead % 2)

    def target(k):
        return (lead - 1 + turn_by * k + others * chips) % others + 1

    def follower(u):
        return target(1 + u // halves), u % halves

    prepare(0, x_ref, w_ref)
    for half in range(halves):
        block(lead, half, first[0], True)

    @pl.when(early_start > 0)
    def _():
        enter()

    for index in (0, 1):
        copies[index].wait_recv()
    prepare(1, other_x, other_w)
    for half in range(halves):
        block(lead, half, first[1], False)
    ahead = jnp.where(gy == 0, FILL0, FILL)
    sweep(ahead, lambda u: block(*follower(u), first[0] + first[1], True))
    for index in (2, 3):
        copies[index].wait_recv()
    prepare_late(0, x_ref, w_ref)
    prepare_late(1, other_x, other_w)

    def send(s, half, places):
        for k in places:
            far(s, half, rank(k)).start()

    def leading(u):
        block(lead, u, late, False)
        send(lead, u, range(1))

    def finish(u):
        s, half = follower(u)
        block(s, half, late, False)
        send(s, half, range(ny - 1))

    def following(u):
        s, half = follower(u)
        block(s, half, first[0] + first[1] + late, True)
        send(s, half, range(ny - 1))

    def own(half):
        block(0, half, first[0] + first[1] + late, True)

    for half in range(halves):
        block(lead, half, late, False)

    @pl.when(place < chips - 1)
    def _():
        pl.semaphore_wait(joined.at[0], chips - 1 - place)

    for k in range(ny - 1):
        for half in range(halves):
            send(lead, half, [k])
    sweep(ahead, finish)
    lax.fori_loop(ahead, halves * (others - 1), lambda u, carry: (following(u), carry)[1], 0)
    for half in range(halves):
        send(lead, half, [ny - 1])
    sweep(halves * (others - 1), lambda u: send(*follower(u), [ny - 1]))
    sweep(halves, own)

    @pl.when(gy < ny - 1)
    def _():
        pl.semaphore_wait(joined.at[1], ny - 1 - gy)

    for k in range(ny):
        z = rank(k)
        for half in range(halves):
            all_of(landed.at[half, z], far_send.at[0], far_recv.at[half, z]).wait_recv()
            total = sums[0, half, rows_of(z), :]
            for s in range(others):
                total = total + landed[half, z, s]
            line[half, z] = total
            if k < ny - 1:
                along(half, z).start()
    for copy in copies:
        copy.wait_send()
    all_of(sums.at[1:], far_send.at[0], far_recv.at[0, 0]).wait_send()
    arrived = all_of(line_in, line_send.at[0], line_recv.at[0])
    arrived.wait_recv()
    for half in range(halves):
        total = line[half, gy]
        for t in range(ny - 1):
            total = total + line_in[t, half]
        for i in range(unit):
            out_ref[half * unit + i] = total[:, i * modes : (i + 1) * modes]
    arrived.wait_send()


def per_device(modes, weights):
    mode_count, cells = modes.shape[1:]
    nx, ny = lax.axis_size("gx"), lax.axis_size("gy")
    _, _, plane, pack, unit, halves, stages = sizes(nx, ny, mode_count, cells)
    factor = 0.5 / math.sqrt(cells * nx * ny)
    rows = 3 * mode_count
    own_i, own_j = mode_count // nx, mode_count // ny
    edge = (rows // pack + 8, plane * pack)
    depth = 2 * stages * cells + 4 * plane
    wide = unit * mode_count
    vmem = pl.BlockSpec(memory_space=pltpu.VMEM)
    chips = nx // 2
    near_count = 4
    return pl.pallas_call(
        functools.partial(kernel, nx, ny, mode_count, factor),
        out_shape=jax.ShapeDtypeStruct((own_i, own_j, mode_count), jnp.float32),
        in_specs=[pl.BlockSpec(memory_space=pltpu.HBM)] * 2,
        out_specs=vmem,
        scratch_shapes=[
            pltpu.VMEM((rows, cells), jnp.float32),
            pltpu.VMEM((1, cells), jnp.float32),
            pltpu.VMEM((rows, cells), jnp.float32),
            pltpu.VMEM((1, cells), jnp.float32),
            pltpu.VMEM(edge, jnp.float32),
            pltpu.VMEM((2, *edge), jnp.float32),
            pltpu.VMEM((nx * halves, 3, unit, 2 * cells + 4 * plane), jnp.float32),
            pltpu.VMEM((3, mode_count, depth), jnp.float32),
            pltpu.VMEM((2 * mode_count, depth), jnp.bfloat16),
            pltpu.VMEM((chips, halves, mode_count, wide), jnp.float32),
            pltpu.VMEM((halves, ny, chips - 1, own_j, wide), jnp.float32),
            pltpu.VMEM((halves, ny, own_j, wide), jnp.float32),
            pltpu.VMEM((ny - 1, halves, own_j, wide), jnp.float32),
            pltpu.SemaphoreType.REGULAR((2,)),
            pltpu.SemaphoreType.DMA((2,)),
            pltpu.SemaphoreType.DMA((near_count,)),
            pltpu.SemaphoreType.DMA((near_count,)),
            pltpu.SemaphoreType.DMA((1,)),
            pltpu.SemaphoreType.DMA((halves, ny)),
            pltpu.SemaphoreType.DMA((1,)),
            pltpu.SemaphoreType.DMA((1,)),
        ],
        compiler_params=pltpu.CompilerParams(collective_id=0, has_side_effects=True, vmem_limit_bytes=24 << 20),
        name="tensor",
    )(pltpu.with_memory_space_constraint(modes.reshape(rows, cells), pltpu.HBM), pltpu.with_memory_space_constraint(weights.reshape(1, cells), pltpu.HBM))


def solution(mesh):
    return jax.shard_map(
        per_device,
        mesh=mesh,
        in_specs=(P(None, None, ("gx", "gy")), P(("gx", "gy"))),
        out_specs=P("gx", "gy", None),
        check_vma=False,
    )
```

```python
import functools
import math

import jax
import jax.numpy as jnp
from jax import lax
from jax.experimental import pallas as pl
from jax.experimental.pallas import tpu as pltpu
from jax.sharding import PartitionSpec as P

CX = 1
CY = 2
LANES = 128
ROWS = 16
UNIT = 4
FILL0 = 2
FILL = 1
MESH = pl.DeviceIdType.MESH


def partner_of(gx):
    return gx + 1 - 2 * (gx % 2)


def split(value):
    high = value.astype(jnp.bfloat16)
    low = (value - high.astype(jnp.float32)).astype(jnp.bfloat16)
    return high, low


def sizes(nx, ny, modes, cells):
    width, height = CX * nx, CY * ny
    plane = width * height
    own_i = modes // nx
    unit = UNIT if own_i % UNIT == 0 else own_i
    stages = 3 if cells > plane else 2
    return width, height, plane, max(1, LANES // plane), unit, own_i // unit, stages


def kernel(
    nx, ny, modes, factor,
    x_in, w_in, out_ref,
    x_ref, w_ref, other_x, other_w, edges, halos, weighted, diffs, field, sums, landed, line, line_in,
    joined, load, near_send, near_recv, far_send, far_recv, line_send, line_recv,
):
    rows, cells = x_ref.shape
    width, height, plane, pack, unit, halves, stages = sizes(nx, ny, modes, cells)
    chips = nx // 2
    devices = nx * ny
    own_j = modes // ny
    early = stages * cells
    part = rows // pack
    gx, gy = lax.axis_index("gx"), lax.axis_index("gy")
    core, place = gx % 2, gx // 2
    mate = (partner_of(gx), gy)
    minor = 2 - chips % 2
    major = chips // minor

    def shifted(s):
        return (place // minor + s // minor) % major * minor + (place % minor + s % minor) % minor

    def beside(step, x, y):
        other = (x * ny + y + step + devices) % devices
        return other // ny, other % ny

    after = beside(1, gx, gy)
    after_mate = (partner_of(after[0]), after[1])
    before = beside(-1, gx, gy)
    before_mate = beside(-1, *mate)

    barrier = pltpu.get_barrier_semaphore()
    loads = [pltpu.make_async_copy(x_in, x_ref, load.at[0]), pltpu.make_async_copy(w_in, w_ref, load.at[1])]
    for copy in loads:
        copy.start()
    for device in (mate, before, before_mate):
        pl.semaphore_signal(barrier, inc=1, device_id=device, device_id_type=MESH)

    def greet(semaphore, sign):
        for q in range(chips):

            @pl.when((q - place) * sign > 0)
            def _():
                pl.semaphore_signal(semaphore[0], inc=1, device_id=(q * 2 + core, gy), device_id_type=MESH)

        for z in range(ny):

            @pl.when((z - gy) * sign > 0)
            def _():
                pl.semaphore_signal(semaphore[1], inc=1, device_id=(gx, z), device_id_type=MESH)

    greet((barrier, barrier), 1)
    for copy in loads:
        copy.wait()

    def turned(value, step):
        span = value.shape[1]
        shift = (-step) % span
        return pltpu.roll(value, shift, 1) if shift else value

    start = cells - plane
    if pack == 1:
        edges[:rows] = x_ref[:, start:]
        edges[rows:] = jnp.broadcast_to(w_ref[:, start:], (8, plane))
    else:
        base = start // LANES * LANES
        lane = lax.broadcasted_iota(jnp.int32, (part, LANES), 1)
        packed = jnp.zeros((part, LANES), jnp.float32)
        for p in range(pack):
            piece = turned(x_ref[p * part : (p + 1) * part, base : base + LANES], start - base - p * plane)
            packed = jnp.where(lane // plane == p, piece, packed)
        edges[:part] = packed
        edges[part:] = jnp.broadcast_to(turned(w_ref[:, base : base + LANES], start - base), (8, LANES))

    def near(index, src, dst, device):
        return pltpu.make_async_remote_copy(
            src_ref=src, dst_ref=dst, send_sem=near_send.at[index], recv_sem=near_recv.at[index],
            device_id=device, device_id_type=MESH,
        )

    copies = [
        near(0, w_in, other_w, mate),
        near(1, x_in, other_x, mate),
        near(2, edges, halos.at[0], after),
        near(3, edges, halos.at[1], after_mate),
    ]
    def enter():
        pl.semaphore_wait(barrier, 3 + place + gy)
        for index in (2, 3, 1, 0):
            copies[index].start()
        greet((joined.at[0], joined.at[1]), -1)

    early_start = 1 - (gy + ny - 1) // ny

    @pl.when(early_start == 0)
    def _():
        enter()


    span = max(plane, LANES)
    lane = lax.broadcasted_iota(jnp.int32, (modes, span), 1)
    at_x, at_y = lane % width, lane // width % height
    whole = lax.broadcasted_iota(jnp.int32, (modes, cells), 1)

    def keep(a, value, weight, scale_at, field_at):
        size = value.shape[1]
        scaled = value * weight
        for n in range(nx * halves):
            weighted[n, a, :, scale_at : scale_at + size] = scaled[n * unit : (n + 1) * unit]
        for at in field_at:
            high, low = split(value)
            field[:modes, at : at + size] = high
            field[modes:, at : at + size] = low

    def across(value, at, count, step):
        turn = (count - 1) * step
        if span == LANES:
            up = jnp.take_along_axis(value, jnp.where(at == count - 1, lane - turn, lane + step), axis=1)
            down = jnp.take_along_axis(value, jnp.where(at == 0, lane + turn, lane - step), axis=1)
        else:
            up = jnp.where(at == count - 1, turned(value, -turn), turned(value, step))
            down = jnp.where(at == 0, turned(value, turn), turned(value, -step))
        return up - down

    def prepare(which, ref, weight_ref):
        for a in range(3):
            for c in range(0, cells, span):
                value = ref[a * modes : (a + 1) * modes, c : c + span]
                at = which * early + c
                weight = weight_ref[:, c : c + span] * factor
                keep(a, value, weight, which * cells + c, [at + a * cells] if a < stages else [])
                diffs[a, :, at : at + span] = across(value, at_x, width, 1)
                diffs[a, :, at + cells : at + cells + span] = across(value, at_y, height, width)
            if stages == 3:
                value = ref[a * modes : (a + 1) * modes, :]
                up = jnp.where(whole < cells - plane, turned(value, plane), 0.0)
                down = jnp.where(whole >= plane, turned(value, -plane), 0.0)
                at = which * early + 2 * cells
                diffs[a, :, at : at + cells] = up - down

    def prepare_late(which, ref, weight_ref):
        at, scale_at = 2 * early + which * 2 * plane, 2 * cells + which * 2 * plane
        if pack == 1:
            for a in range(3):
                mine = slice(a * modes, (a + 1) * modes)
                own, halo = ref[mine, :plane], halos[which, mine, :]
                for value, other, weight, step in (
                    (own, -halo, weight_ref[:, :plane], 0),
                    (halo, own, halos[which, rows : rows + 1, :], plane),
                ):
                    keep(a, value, weight * factor, scale_at + step, [at + step] if a == 2 else [])
                    diffs[a, :, at + step : at + step + plane] = other
            return
        narrow = lax.broadcasted_iota(jnp.int32, (8, LANES), 1)
        low_part = narrow < plane
        weight = jnp.where(low_part[:1], weight_ref[:, :LANES], turned(halos[which, part : part + 1, :], -plane))
        for a in range(3):
            values = []
            for r in range(0, modes, 8):
                q = a * modes + r
                own = ref[q : q + 8, :LANES]
                halo = halos[which, q % part : q % part + 8, :]
                halo = turned(halo, (q // part - 1) * plane)
                values.append(jnp.where(low_part, own, halo))
                diffs[a, r : r + 8, at : at + LANES] = turned(jnp.where(low_part, own, -halo), plane)
            keep(a, jnp.concatenate(values, axis=0), weight * factor, scale_at, [at] if a == 2 else [])

    dims = (((1,), (1,)), ((), ()))
    first = [
        [(which * early + b * cells + c, which * cells + c) for b in range(stages) for c in range(0, cells, LANES)]
        for which in range(2)
    ]
    late = [(2 * early + c, 2 * cells + c) for c in range(0, 4 * plane, LANES)]

    def block(s, half, tiles, fresh):
        group = (shifted(s) * 2 + core) * halves + half
        highs, lows = [], []
        for i in range(unit):
            for k in range(0, modes, ROWS):
                pieces = []
                for at, scale_at in tiles:
                    scales = [
                        weighted[group, a, i : i + 1, scale_at : scale_at + LANES] for a in range(3)
                    ]
                    value = scales[0] * diffs[0, k : k + ROWS, at : at + LANES]
                    for a in (1, 2):
                        value = value + scales[a] * diffs[a, k : k + ROWS, at : at + LANES]
                    pieces.append(split(value))
                highs.append(jnp.concatenate([piece[0] for piece in pieces], axis=1))
                lows.append(jnp.concatenate([piece[1] for piece in pieces], axis=1))
        high, low = jnp.concatenate(highs, axis=0), jnp.concatenate(lows, axis=0)
        columns = slice(tiles[0][0], tiles[-1][0] + LANES)
        main = lax.dot_general(field[:, columns], high, dims, preferred_element_type=jnp.float32)
        rest = lax.dot_general(field[:modes, columns], low, dims, preferred_element_type=jnp.float32)
        value = main[:modes] + (main[modes:] + rest)
        sums[s, half] = value if fresh else sums[s, half] + value

    def rank(k):
        if k == ny - 1:
            return gy
        return k + (k - gy + ny) // ny

    def rows_of(z):
        return pl.ds(pl.multiple_of(z * own_j, own_j), own_j)

    def far(s, half, z):
        return pltpu.make_async_remote_copy(
            src_ref=sums.at[s, half, rows_of(z), :], dst_ref=landed.at[half, z, s - 1],
            send_sem=far_send.at[0], recv_sem=far_recv.at[half, z],
            device_id=(shifted(s) * 2 + core, gy), device_id_type=MESH,
        )

    def along(half, z):
        slot = (gy - z + ny) % ny - 1
        return pltpu.make_async_remote_copy(
            src_ref=line.at[half, z], dst_ref=line_in.at[slot, half],
            send_sem=line_send.at[0], recv_sem=line_recv.at[0],
            device_id=(gx, z), device_id_type=MESH,
        )

    def all_of(ref, send_sem, recv_sem):
        return pltpu.make_async_remote_copy(
            src_ref=ref, dst_ref=ref, send_sem=send_sem, recv_sem=recv_sem,
            device_id=mate, device_id_type=MESH,
        )

    def sweep(count, body):
        def step(u, carry):
            body(u)
            return carry

        lax.fori_loop(0, count, step, 0)

    others = chips - 1
    home = -(place // minor) % major * minor + -(place % minor) % minor
    lead = home + others * (1 - (home + others) // chips)
    turn_by = 1 - 2 * (lead % 2)

    def target(k):
        return (lead - 1 + turn_by * k + others * chips) % others + 1

    def follower(u):
        return target(1 + u // halves), u % halves

    prepare(0, x_ref, w_ref)
    for half in range(halves):
        block(lead, half, first[0], True)

    @pl.when(early_start > 0)
    def _():
        enter()

    for index in (0, 1):
        copies[index].wait_recv()
    prepare(1, other_x, other_w)
    for half in range(halves):
        block(lead, half, first[1], False)
    ahead = jnp.where(gy == 0, FILL0, FILL)
    sweep(ahead, lambda u: block(*follower(u), first[0] + first[1], True))
    copies[2].wait_recv()
    prepare_late(0, x_ref, w_ref)
    copies[3].wait_recv()
    prepare_late(1, other_x, other_w)

    def send(s, half, places):
        for k in places:
            far(s, half, rank(k)).start()

    def leading(u):
        block(lead, u, late, False)
        send(lead, u, range(1))

    def finish(u):
        s, half = follower(u)
        block(s, half, late, False)
        send(s, half, range(ny - 1))

    def following(u):
        s, half = follower(u)
        block(s, half, first[0] + first[1] + late, True)
        send(s, half, range(ny - 1))

    def own(half):
        block(0, half, first[0] + first[1] + late, True)

    for half in range(halves):
        block(lead, half, late, False)

    @pl.when(place < chips - 1)
    def _():
        pl.semaphore_wait(joined.at[0], chips - 1 - place)

    for k in range(ny - 1):
        for half in range(halves):
            send(lead, half, [k])
    sweep(ahead, finish)
    lax.fori_loop(ahead, halves * (others - 1), lambda u, carry: (following(u), carry)[1], 0)
    for half in range(halves):
        send(lead, half, [ny - 1])
    sweep(halves, own)
    sweep(halves * (others - 1), lambda u: send(*follower(u), [ny - 1]))

    @pl.when(gy < ny - 1)
    def _():
        pl.semaphore_wait(joined.at[1], ny - 1 - gy)

    for k in range(ny):
        z = rank(k)
        for half in range(halves):
            all_of(landed.at[half, z], far_send.at[0], far_recv.at[half, z]).wait_recv()
            total = sums[0, half, rows_of(z), :]
            for s in range(others):
                total = total + landed[half, z, s]
            line[half, z] = total
            if k < ny - 1:
                along(half, z).start()
    for copy in copies:
        copy.wait_send()
    all_of(sums.at[1:], far_send.at[0], far_recv.at[0, 0]).wait_send()
    arrived = all_of(line_in, line_send.at[0], line_recv.at[0])
    arrived.wait_recv()
    for half in range(halves):
        total = line[half, gy]
        for t in range(ny - 1):
            total = total + line_in[t, half]
        for i in range(unit):
            out_ref[half * unit + i] = total[:, i * modes : (i + 1) * modes]
    arrived.wait_send()


def per_device(modes, weights):
    mode_count, cells = modes.shape[1:]
    nx, ny = lax.axis_size("gx"), lax.axis_size("gy")
    _, _, plane, pack, unit, halves, stages = sizes(nx, ny, mode_count, cells)
    factor = 0.5 / math.sqrt(cells * nx * ny)
    rows = 3 * mode_count
    own_i, own_j = mode_count // nx, mode_count // ny
    edge = (rows // pack + 8, plane * pack)
    depth = 2 * stages * cells + 4 * plane
    wide = unit * mode_count
    vmem = pl.BlockSpec(memory_space=pltpu.VMEM)
    chips = nx // 2
    near_count = 4
    return pl.pallas_call(
        functools.partial(kernel, nx, ny, mode_count, factor),
        out_shape=jax.ShapeDtypeStruct((own_i, own_j, mode_count), jnp.float32),
        in_specs=[pl.BlockSpec(memory_space=pltpu.HBM)] * 2,
        out_specs=vmem,
        scratch_shapes=[
            pltpu.VMEM((rows, cells), jnp.float32),
            pltpu.VMEM((1, cells), jnp.float32),
            pltpu.VMEM((rows, cells), jnp.float32),
            pltpu.VMEM((1, cells), jnp.float32),
            pltpu.VMEM(edge, jnp.float32),
            pltpu.VMEM((2, *edge), jnp.float32),
            pltpu.VMEM((nx * halves, 3, unit, 2 * cells + 4 * plane), jnp.float32),
            pltpu.VMEM((3, mode_count, depth), jnp.float32),
            pltpu.VMEM((2 * mode_count, depth), jnp.bfloat16),
            pltpu.VMEM((chips, halves, mode_count, wide), jnp.float32),
            pltpu.VMEM((halves, ny, chips - 1, own_j, wide), jnp.float32),
            pltpu.VMEM((halves, ny, own_j, wide), jnp.float32),
            pltpu.VMEM((ny - 1, halves, own_j, wide), jnp.float32),
            pltpu.SemaphoreType.REGULAR((2,)),
            pltpu.SemaphoreType.DMA((2,)),
            pltpu.SemaphoreType.DMA((near_count,)),
            pltpu.SemaphoreType.DMA((near_count,)),
            pltpu.SemaphoreType.DMA((1,)),
            pltpu.SemaphoreType.DMA((halves, ny)),
            pltpu.SemaphoreType.DMA((1,)),
            pltpu.SemaphoreType.DMA((1,)),
        ],
        compiler_params=pltpu.CompilerParams(collective_id=0, has_side_effects=True, vmem_limit_bytes=24 << 20),
        name="tensor",
    )(pltpu.with_memory_space_constraint(modes.reshape(rows, cells), pltpu.HBM), pltpu.with_memory_space_constraint(weights.reshape(1, cells), pltpu.HBM))


def solution(mesh):
    return jax.shard_map(
        per_device,
        mesh=mesh,
        in_specs=(P(None, None, ("gx", "gy")), P(("gx", "gy"))),
        out_specs=P("gx", "gy", None),
        check_vma=False,
    )
```
